1024 devices in a mesh: ctx: 128 (over z, x), tensor: 8 (over y, core).
Axes of the slice: x: 4, y: 4, z: 32, core: 2. Of those that a mesh axis runs over, the one named last changes fastest.
Arguments:
- queries: bfloat16 [49152, 8192], P('ctx', 'tensor'), may hold values from -64 to 64
- key_layout_rows: bfloat16 [49152, 1024], P('ctx', 'tensor'), may hold values from -5 to 5
- value_layout_rows: bfloat16 [49152, 1024], P('ctx', 'tensor'), may hold values from -6 to 6
- output_gradient: bfloat16 [49152, 8192], P('ctx', 'tensor'), may hold values from -6 to 6
- doc_starts: int32 [384], P('ctx'), may hold values from 0 to 1, as said below
- block_mapping: int32 [384], replicated, may hold values from 0 to 383, as said below
Outputs:
- query_grad: bfloat16 [49152, 8192], P(('ctx', 'tensor'))
- key_grad: bfloat16 [49152, 1024], P(('ctx', 'tensor'))
- value_grad: bfloat16 [49152, 1024], P(('ctx', 'tensor'))
The draws below stay inside these ranges and needn't reach their ends.
Inputs may be any that keep to these rules, and one draw needn't show every extreme that they name: `doc_starts`: the first block of every index of ctx begins a document, so in the executing layout every document lies whole within the 384 tokens of one index of ctx. A permutation of the blocks. Block s lies on index s // 3 of ctx; block_mapping[s] lies on that index or on the index 64 away. At least one and at most 2 blocks of each index come from the other index of its pair; indices 0 and 64 take exactly 2.
All inputs are finite; a program needn't handle non-finite values.
Results may differ from the reference program's by a relative error of at most 0.006.
Values may be sent and summed in bfloat16 or wider, within the bound.
A program may use at most 32 MiB of HBM per device.

```python
import jax
import jax.numpy as jnp
from jax import lax

QUERY_HEADS = 64
KEY_VALUE_HEADS = 8
HEAD_SIZE = 128
TOKENS_PER_SHARD = 384
BLK = 128
NBLK = 3
CAP = 2
TOKEN_COUNT = 49152
NBLOCKS = 384
N_CTX = 128


def draw_key_layout_rows(key, part):
    drawn = jax.random.normal(jax.random.fold_in(key, 101), (TOKEN_COUNT, KEY_VALUE_HEADS * HEAD_SIZE), jnp.float32)
    return jnp.clip(drawn, -5.0, 5.0).astype(jnp.bfloat16)


def draw_queries(key, part):
    drawn = jax.random.normal(jax.random.fold_in(key, 102), (TOKEN_COUNT, QUERY_HEADS * HEAD_SIZE), jnp.float32)
    return jnp.clip(drawn, -5.0, 5.0).astype(jnp.bfloat16)


def draw_doc_starts(key, part):
    flags = jax.random.randint(jax.random.fold_in(key, 7), (N_CTX, NBLK), 0, 2, jnp.int32)
    flags = flags.at[:, 0].set(1)
    return flags.reshape(NBLOCKS).astype(jnp.int32)


def draw_block_mapping(key, part):
    half_axis = N_CTX // 2
    moved_counts = jax.random.randint(jax.random.fold_in(key, 12), (half_axis,), 1, CAP + 1, jnp.int32)
    moved_counts = moved_counts.at[0].set(CAP)
    pair_keys = jax.random.split(jax.random.fold_in(key, 11), half_axis)

    def one_pair(pair_key, moved, first):
        key_one, key_two, key_three, key_four = jax.random.split(pair_key, 4)
        order_first = jax.random.permutation(key_one, NBLK).astype(jnp.int32)
        order_second = jax.random.permutation(key_two, NBLK).astype(jnp.int32)
        slot_ids = jnp.arange(NBLK, dtype=jnp.int32)
        base_first = first * NBLK
        base_second = (first + half_axis) * NBLK
        takes_first = jnp.where(slot_ids < moved, base_second + order_second, base_first + order_first)
        takes_second = jnp.where(slot_ids < moved, base_first + order_first, base_second + order_second)
        shuffle_first = jax.random.permutation(key_three, NBLK)
        shuffle_second = jax.random.permutation(key_four, NBLK)
        return (takes_first[shuffle_first], takes_second[shuffle_second])
    rows_first, rows_second = jax.vmap(one_pair)(pair_keys, moved_counts, jnp.arange(half_axis, dtype=jnp.int32))
    return jnp.concatenate([rows_first, rows_second], axis=0).reshape(NBLOCKS).astype(jnp.int32)


def level_of(stream_key, shape, shards, least, largest):
    factor_of = 1.0
    for dim, parts in shards:
        steps = jax.random.uniform(jax.random.fold_in(jax.random.fold_in(stream_key, 6), dim), (parts,), jnp.float32, least / len(shards), largest / len(shards))
        factor_of = factor_of * jnp.repeat(jnp.exp(steps), shape[dim] // parts).reshape((-1,) + (1,) * (len(shape) - 1 - dim))
    return factor_of


def noise(rng, extent, spread, limit, cuts=(), held_as=jnp.bfloat16):
    entries = spread * jax.random.normal(rng, extent, jnp.float32)
    if cuts:
        entries = entries * level_of(rng, extent, cuts, -0.22, 0.18)
    return jnp.clip(entries, -limit, limit).astype(held_as)


def setup_inputs(seed: int = 0) -> dict:
    key_list = jax.random.split(jax.random.key(seed), 7)
    return {
        "queries": draw_queries(jax.random.fold_in(key_list[6], 71), 0),
        "key_layout_rows": draw_key_layout_rows(jax.random.fold_in(key_list[6], 71), 0),
        "value_layout_rows": noise(key_list[2], (TOKEN_COUNT, KEY_VALUE_HEADS * HEAD_SIZE), 1.0, 6.0, ((0, 128), (1, 8))),
        "output_gradient": noise(key_list[3], (TOKEN_COUNT, QUERY_HEADS * HEAD_SIZE), 1.0, 6.0, ((0, 128), (1, 8))),
        "doc_starts": draw_doc_starts(jax.random.fold_in(key_list[6], 71), 0),
        "block_mapping": draw_block_mapping(jax.random.fold_in(key_list[6], 71), 0),
    }


def rounded(values):
    return lax.optimization_barrier(values.astype(jnp.bfloat16)).astype(jnp.float32)


def device_grads(inputs):
    queries, key_layout_rows, value_layout_rows, output_gradient, starts = inputs
    head_repeats = QUERY_HEADS // KEY_VALUE_HEADS
    scaling = HEAD_SIZE ** -0.5
    document = jnp.repeat(jnp.cumsum(starts).astype(jnp.int32), BLK)
    position = jnp.arange(TOKENS_PER_SHARD, dtype=jnp.int32)
    visible = (document[:, None] == document[None, :]) & (position[:, None] >= position[None, :])
    query_expanded = queries.astype(jnp.float32).reshape(TOKENS_PER_SHARD, KEY_VALUE_HEADS, head_repeats, HEAD_SIZE)
    gradient_expanded = output_gradient.astype(jnp.float32).reshape(TOKENS_PER_SHARD, KEY_VALUE_HEADS, head_repeats, HEAD_SIZE)
    key_expanded = key_layout_rows.astype(jnp.float32).reshape(TOKENS_PER_SHARD, KEY_VALUE_HEADS, HEAD_SIZE)
    value_expanded = value_layout_rows.astype(jnp.float32).reshape(TOKENS_PER_SHARD, KEY_VALUE_HEADS, HEAD_SIZE)
    scores = jnp.einsum("qgrd,kgd->grqk", query_expanded, key_expanded) * scaling
    row_top = jnp.max(jnp.where(visible, scores, -1e30), axis=-1, keepdims=True)
    weights = jnp.where(visible, jnp.exp(scores - row_top), 0.0)
    weights = weights / jnp.sum(weights, axis=-1, keepdims=True)
    dprobs = jnp.einsum("qgrd,kgd->grqk", gradient_expanded, value_expanded)
    row_delta = jnp.sum(weights * dprobs, axis=-1, keepdims=True)
    value_running = jnp.einsum("grqk,qgrd->kgd", rounded(weights), gradient_expanded)
    dscores = rounded(weights * (dprobs - row_delta))
    query_exec = jnp.einsum("grqk,kgd->qgrd", dscores, key_expanded) * scaling
    key_running = jnp.einsum("grqk,qgrd->kgd", dscores, query_expanded) * scaling
    return (query_exec.reshape(TOKENS_PER_SHARD, QUERY_HEADS * HEAD_SIZE).astype(jnp.bfloat16),
            key_running.reshape(TOKENS_PER_SHARD, KEY_VALUE_HEADS * HEAD_SIZE).astype(jnp.bfloat16),
            value_running.reshape(TOKENS_PER_SHARD, KEY_VALUE_HEADS * HEAD_SIZE).astype(jnp.bfloat16))


def return_to_owner(gradients, block_mapping):
    columns = gradients.shape[-1]
    blocks = gradients.reshape(NBLOCKS, BLK, columns)
    owned = jnp.zeros_like(blocks).at[block_mapping].set(blocks)
    return owned.reshape(TOKEN_COUNT, columns)


def reference(queries, key_layout_rows, value_layout_rows, output_gradient, doc_starts, block_mapping):
    stacked = (queries.reshape(N_CTX, TOKENS_PER_SHARD, QUERY_HEADS * HEAD_SIZE),
               key_layout_rows.reshape(N_CTX, TOKENS_PER_SHARD, KEY_VALUE_HEADS * HEAD_SIZE),
               value_layout_rows.reshape(N_CTX, TOKENS_PER_SHARD, KEY_VALUE_HEADS * HEAD_SIZE),
               output_gradient.reshape(N_CTX, TOKENS_PER_SHARD, QUERY_HEADS * HEAD_SIZE),
               doc_starts.reshape(N_CTX, NBLK))
    query_exec, key_running, value_running = lax.map(device_grads, stacked)
    return (return_to_owner(query_exec.reshape(TOKEN_COUNT, QUERY_HEADS * HEAD_SIZE), block_mapping),
            return_to_owner(key_running.reshape(TOKEN_COUNT, KEY_VALUE_HEADS * HEAD_SIZE), block_mapping),
            return_to_owner(value_running.reshape(TOKEN_COUNT, KEY_VALUE_HEADS * HEAD_SIZE), block_mapping))
```

```python
import jax
import jax.numpy as jnp
from jax import lax
from jax.experimental import pallas as pl
from jax.experimental.pallas import tpu as pltpu
from jax.sharding import PartitionSpec as P

HEAD_SIZE = 128
HIDDEN = -1e30
NT = (((1,), (1,)), ((), ()))
NN = (((1,), (0,)), ((), ()))


def product(a, b, dims):
    return lax.dot_general(a, b, dims, preferred_element_type=jnp.float32)


def stacked_heads(ref, rows, columns, heads):
    tile = ref[rows, columns]
    return jnp.concatenate(
        [tile[:, h * HEAD_SIZE : (h + 1) * HEAD_SIZE] for h in range(heads)], axis=0
    )


def attention_kernel(starts_ref, q_ref, k_ref, v_ref, g_ref, out_ref, key_acc, value_acc):
    block_count, block_rows, _ = out_ref.shape
    query_cols = q_ref.shape[1]
    heads = 2
    width = heads * HEAD_SIZE
    lanes = heads * block_rows
    scaling = HEAD_SIZE ** (-0.5)
    key_pos = lax.broadcasted_iota(jnp.int32, (block_rows, lanes), 0)
    query_pos = lax.broadcasted_iota(jnp.int32, (block_rows, lanes), 1) % block_rows
    causal = query_pos >= key_pos
    bias = {}
    for i in range(block_count):
        crossed = jnp.int32(0)
        for j in range(i - 1, -1, -1):
            crossed = crossed + starts_ref[j + 1]
            bias[i, j] = jnp.where(crossed == 0, 0.0, HIDDEN).astype(jnp.float32)
    key_rows = k_ref[...]
    value_rows = v_ref[...]
    key_turned = key_rows.astype(jnp.float32).T.astype(jnp.bfloat16)
    key_acc[...] = jnp.zeros_like(key_acc)
    value_acc[...] = jnp.zeros_like(value_acc)

    def head_pair(pair, carried):
        columns = pl.ds(pl.multiple_of(pair * width, width), width)
        for i in range(block_count):
            seen = (i + 1) * block_rows
            rows = slice(i * block_rows, seen)
            query = stacked_heads(q_ref, rows, columns, heads)
            grad = stacked_heads(g_ref, rows, columns, heads)
            scores = product(key_rows[:seen], query, NT) * scaling
            dprobs = product(value_rows[:seen], grad, NT)
            masked = [
                scores[j * block_rows : (j + 1) * block_rows] + bias[i, j] for j in range(i)
            ] + [jnp.where(causal, scores[rows], HIDDEN)]
            scores = jnp.concatenate(masked, axis=0)
            raised = jnp.exp(scores - jnp.max(scores, axis=0, keepdims=True))
            weights = raised * (1.0 / jnp.sum(raised, axis=0, keepdims=True))
            delta = jnp.sum(weights * dprobs, axis=0, keepdims=True)
            weights_low = weights.astype(jnp.bfloat16)
            dscores = (weights * (dprobs - delta)).astype(jnp.bfloat16)
            value_acc[:seen, :] += product(weights_low, grad, NN)
            key_acc[:seen, :] += product(dscores, query, NN)
            turned = product(key_turned[:, :seen], dscores, NN) * scaling
            dquery = jnp.concatenate(
                [
                    turned[:, h * block_rows : (h + 1) * block_rows].T
                    for h in range(heads)
                ],
                axis=1,
            )
            out_ref[i, :, columns] = dquery.astype(jnp.bfloat16)
        return carried

    lax.fori_loop(0, query_cols // width, head_pair, 0)
    for i in range(block_count):
        rows = slice(i * block_rows, (i + 1) * block_rows)
        out_ref[i, :, query_cols : query_cols + HEAD_SIZE] = (
            key_acc[rows, :] * scaling
        ).astype(jnp.bfloat16)
        out_ref[i, :, query_cols + HEAD_SIZE : query_cols + 2 * HEAD_SIZE] = value_acc[
            rows, :
        ].astype(jnp.bfloat16)


def attention_blocks(queries, keys, values, grads, starts):
    rows, query_cols = queries.shape
    block_count = starts.shape[0]
    vmem = pl.BlockSpec(memory_space=pltpu.VMEM)
    return pl.pallas_call(
        attention_kernel,
        out_shape=jax.ShapeDtypeStruct(
            (block_count, rows // block_count, query_cols + 2 * HEAD_SIZE), jnp.bfloat16
        ),
        in_specs=[pl.BlockSpec(memory_space=pltpu.SMEM)] + [vmem] * 4,
        out_specs=vmem,
        scratch_shapes=[pltpu.VMEM((rows, HEAD_SIZE), jnp.float32)] * 2,
        name="attention",
    )(starts, queries, keys, values, grads)


def block_plan(block_mapping, block_count, cap):
    axis_length = lax.axis_size("ctx")
    position = lax.axis_index("ctx")
    partner = (position + axis_length // 2) % axis_length
    own_plan = lax.dynamic_slice_in_dim(block_mapping, position * block_count, block_count)
    peer_plan = lax.dynamic_slice_in_dim(block_mapping, partner * block_count, block_count)
    slots = jnp.arange(block_count, dtype=jnp.int32)
    picks = jnp.arange(cap, dtype=jnp.int32)
    leaves = (own_plan // block_count != position).astype(jnp.int32)
    leave_rank = jnp.cumsum(leaves) - leaves
    sent = jnp.sum(
        ((leaves[None, :] == 1) & (leave_rank[None, :] == picks[:, None])) * slots[None, :], axis=1
    ).astype(jnp.int32)
    comes = (peer_plan // block_count == position).astype(jnp.int32)
    come_rank = jnp.cumsum(comes) - comes
    wanted = position * block_count + slots
    own_match = (own_plan[:, None] == wanted[None, :]).astype(jnp.int32)
    peer_match = (peer_plan[:, None] == wanted[None, :]).astype(jnp.int32)
    source = jnp.sum(own_match * slots[:, None], axis=0) + jnp.sum(
        peer_match * (block_count + come_rank)[:, None], axis=0
    )
    return jnp.sum(leaves), sent, source.astype(jnp.int32)


def on_device(
    queries, key_layout_rows, value_layout_rows, output_gradient, doc_starts, block_mapping
):
    rows_dev, query_cols = queries.shape
    block_count = doc_starts.shape[0]
    cap = 2
    blocks = attention_blocks(
        queries, key_layout_rows, value_layout_rows, output_gradient, doc_starts
    )
    moved, sent, source = block_plan(block_mapping, block_count, cap)
    axis_length = lax.axis_size("ctx")
    outgoing = jnp.take(blocks, sent, axis=0)
    across = [(i, (i + axis_length // 2) % axis_length) for i in range(axis_length)]

    def exchange(count):
        def branch(operands):
            blocks, outgoing, source = operands
            arrived = lax.ppermute(outgoing[:count], "ctx", across)
            return jnp.take(jnp.concatenate([blocks, arrived], axis=0), source, axis=0)

        return branch

    owned = lax.switch(
        moved - 1,
        [exchange(count + 1) for count in range(cap)],
        (blocks, outgoing, source),
    ).reshape(rows_dev, -1)
    pieces = (
        owned[:, :query_cols],
        owned[:, query_cols : query_cols + HEAD_SIZE],
        owned[:, query_cols + HEAD_SIZE :],
    )
    return tuple(
        lax.all_to_all(piece, "tensor", split_axis=0, concat_axis=1, tiled=True)
        for piece in pieces
    )


def solution(mesh):
    return jax.shard_map(
        on_device,
        mesh=mesh,
        in_specs=(
            P("ctx", "tensor"),
            P("ctx", "tensor"),
            P("ctx", "tensor"),
            P("ctx", "tensor"),
            P("ctx"),
            P(),
        ),
        out_specs=(
            P(("ctx", "tensor"), None),
            P(("ctx", "tensor"), None),
            P(("ctx", "tensor"), None),
        ),
        check_vma=False,
    )
```

```python
import jax
import jax.numpy as jnp
from jax import lax
from jax.experimental import pallas as pl
from jax.experimental.pallas import tpu as pltpu
from jax.sharding import PartitionSpec as P

HEAD_SIZE = 128
HIDDEN = -1e30
CAP = 2
HEADS = 2
UNROLL = 4
GRANT = 16 * 2**20
NT = (((1,), (1,)), ((), ()))
NN = (((1,), (0,)), ((), ()))
VMEM = pl.BlockSpec(memory_space=pltpu.VMEM)
SMEM = pl.BlockSpec(memory_space=pltpu.SMEM)
MESH = pl.DeviceIdType.MESH


def product(a, b, dims):
    return lax.dot_general(a, b, dims, preferred_element_type=jnp.float32)


def stacked_heads(ref, rows, columns):
    tile = ref[rows, columns]
    return jnp.concatenate(
        [tile[:, h * HEAD_SIZE : (h + 1) * HEAD_SIZE] for h in range(HEADS)], axis=0
    )


def gradients(starts_ref, q_ref, k_ref, v_ref, g_ref, out_ref, key_acc, value_acc):
    query_cols = q_ref.shape[1]
    block_count = starts_ref.shape[0]
    block_rows = q_ref.shape[0] // block_count
    width = HEADS * HEAD_SIZE
    lanes = HEADS * block_rows
    scaling = HEAD_SIZE ** (-0.5)
    key_pos = lax.broadcasted_iota(jnp.int32, (block_rows, lanes), 0)
    query_pos = lax.broadcasted_iota(jnp.int32, (block_rows, lanes), 1) % block_rows
    causal = query_pos >= key_pos
    bias = {}
    for i in range(block_count):
        crossed = jnp.int32(0)
        for j in range(i - 1, -1, -1):
            crossed = crossed + starts_ref[j + 1]
            bias[i, j] = jnp.where(crossed == 0, 0.0, HIDDEN).astype(jnp.float32)
    key_rows = k_ref[...]
    value_rows = v_ref[...]
    key_turned = key_rows.astype(jnp.float32).T.astype(jnp.bfloat16)

    def head_pair(pair, carried):
        columns = pl.ds(pl.multiple_of(pair * width, width), width)
        for i in range(block_count):
            seen = (i + 1) * block_rows
            rows = slice(i * block_rows, seen)
            query = stacked_heads(q_ref, rows, columns)
            grad = stacked_heads(g_ref, rows, columns)
            scores = product(key_rows[:seen], query, NT) * scaling
            dprobs = product(value_rows[:seen], grad, NT)
            masked = [
                scores[j * block_rows : (j + 1) * block_rows] + bias[i, j] for j in range(i)
            ] + [jnp.where(causal, scores[rows], HIDDEN)]
            scores = jnp.concatenate(masked, axis=0)
            raised = jnp.exp(scores - jnp.max(scores, axis=0, keepdims=True))
            weights = raised * (1.0 / jnp.sum(raised, axis=0, keepdims=True))
            delta = jnp.sum(weights * dprobs, axis=0, keepdims=True)
            weights_low = weights.astype(jnp.bfloat16)
            dscores = (weights * (dprobs - delta)).astype(jnp.bfloat16)
            value_acc[:seen, :] += product(weights_low, grad, NN)
            key_acc[:seen, :] += product(dscores, query, NN)
            turned = product(key_turned[:, :seen], dscores, NN) * scaling
            dquery = jnp.concatenate(
                [turned[:, h * block_rows : (h + 1) * block_rows].T for h in range(HEADS)],
                axis=1,
            )
            out_ref[i, :, columns] = dquery.astype(jnp.bfloat16)
        return carried

    lax.fori_loop(0, query_cols // width, head_pair, 0, unroll=UNROLL)
    for i in range(block_count):
        rows = slice(i * block_rows, (i + 1) * block_rows)
        out_ref[i, :, query_cols : query_cols + HEAD_SIZE] = (
            key_acc[rows, :] * scaling
        ).astype(jnp.bfloat16)
        out_ref[i, :, query_cols + HEAD_SIZE :] = value_acc[rows, :].astype(jnp.bfloat16)


def pack(out_ref, packed_ref, plan_ref):
    for j in range(CAP):
        packed_ref[j] = out_ref[plan_ref[1 + j]]


def make_plan(block_count, mapping_ref, plan_ref):
    axis_length = lax.axis_size("ctx")
    position = lax.axis_index("ctx")
    partner = lax.rem(position + axis_length // 2, axis_length)
    zero = jnp.int32(0)
    leaving = zero
    sent = [zero] * CAP
    source = [zero] * block_count
    for s in range(block_count):
        target = mapping_ref[position * block_count + s] - position * block_count
        stays = (target >= 0) & (target < block_count)
        for j in range(CAP):
            sent[j] = jnp.where(stays | (leaving != j), sent[j], s)
        leaving = jnp.where(stays, leaving, leaving + 1)
        for w in range(block_count):
            source[w] = jnp.where(target == w, s, source[w])
    arriving = jnp.int32(block_count)
    for s in range(block_count):
        target = mapping_ref[partner * block_count + s] - position * block_count
        comes = (target >= 0) & (target < block_count)
        for w in range(block_count):
            source[w] = jnp.where(target == w, arriving, source[w])
        arriving = jnp.where(comes, arriving + 1, arriving)
    plan_ref[0] = leaving
    for j in range(CAP):
        plan_ref[1 + j] = sent[j]
    for w in range(block_count):
        plan_ref[1 + CAP + w] = source[w]


def attention_kernel(
    starts_ref, mapping_ref, q_ref, k_ref, v_ref, g_ref,
    out_ref, packed_ref, plan_ref, moved_ref, key_acc, value_acc,
):
    make_plan(starts_ref.shape[0], mapping_ref, plan_ref)
    moved_ref[0] = plan_ref[0] - 1
    key_acc[...] = jnp.zeros_like(key_acc)
    value_acc[...] = jnp.zeros_like(value_acc)
    gradients(starts_ref, q_ref, k_ref, v_ref, g_ref, out_ref, key_acc, value_acc)
    pack(out_ref, packed_ref, plan_ref)


def chosen(own_ref, arrived_ref, place):
    own_count, arrived_count = own_ref.shape[0], arrived_ref.shape[0]
    own = own_ref[jnp.minimum(place, own_count - 1)]
    arrived = arrived_ref[jnp.clip(place - own_count, 0, arrived_count - 1)]
    return jnp.where(place < own_count, own, arrived)


def merge_kernel(plan_ref, own_ref, arrived_ref, out_ref):
    block_count, block_rows, _ = own_ref.shape
    for w in range(block_count):
        rows = slice(w * block_rows, (w + 1) * block_rows)
        out_ref[rows, :] = chosen(own_ref, arrived_ref, plan_ref[1 + CAP + w])


def share_kernel(
    plan_ref, own_ref, arrived_ref, landed_ref,
    stage, relay, near_send, near_recv, first_send, first_recv, last_send, last_recv,
):
    peers, share, columns = landed_ref.shape
    half = columns // 2
    me = lax.axis_index("tensor")
    core = lax.rem(me, 2)
    barrier = pltpu.get_barrier_semaphore()
    for k in range(1, peers):
        pl.semaphore_signal(
            barrier, inc=1, device_id={"tensor": lax.rem(me + k, peers)}, device_id_type=MESH
        )
    merge_kernel(plan_ref, own_ref, arrived_ref, stage)
    pl.semaphore_wait(barrier, peers - 1)

    def device(chips, which):
        return lax.rem(me - core + 2 * chips + peers, peers) + which

    def rows_of(peer):
        return stage.at[pl.ds(pl.multiple_of(peer * share, share), share)]

    def send(source, target, send_sem, recv_sem, to):
        return pltpu.make_async_remote_copy(
            source, target, send_sem, recv_sem, device_id={"tensor": to}, device_id_type=MESH
        )

    ways = ((0, 1), (1, -1))
    cores = (0, 1)
    firsts, nears, lasts = [], [], []
    for w, chips in ways:
        for c in cores:
            firsts.append(
                send(
                    rows_of(device(2, c)).at[:, pl.ds(w * half, half)],
                    relay.at[w, core],
                    first_send.at[w, c],
                    first_recv.at[w, core],
                    device(chips, c),
                )
            )
    for w, chips in ways:
        for c in cores:
            to = device(chips, c)
            nears.append(
                send(rows_of(to), landed_ref.at[me], near_send.at[w, c], near_recv.at[w, core], to)
            )
    other = device(0, 1 - core)
    nears.append(send(rows_of(other), landed_ref.at[me], near_send.at[2, 0], near_recv.at[2, 0], other))
    for copy in firsts + nears:
        copy.start()
    landed_ref[me] = rows_of(me)[...]
    for w, chips in ways:
        for c in cores:
            slot = relay.at[w, c]
            send(slot, slot, first_send.at[w, c], first_recv.at[w, c], other).wait_recv()
            onward = send(
                slot,
                landed_ref.at[device(-chips, c), :, pl.ds(w * half, half)],
                last_send.at[w, c],
                last_recv.at[w, c],
                device(chips, core),
            )
            onward.start()
            lasts.append(onward)
    for copy in firsts + nears + lasts:
        copy.wait_send()
    whole = landed_ref.at[me]
    for w, _ in ways:
        for c in cores:
            send(whole, whole, near_send.at[w, c], near_recv.at[w, c], other).wait_recv()
            send(relay.at[w, c], relay.at[w, c], last_send.at[w, c], last_recv.at[w, c], other).wait_recv()
    send(whole, whole, near_send.at[2, 0], near_recv.at[2, 0], other).wait_recv()


def assemble_kernel(landed_ref, query_ref, key_ref, value_ref):
    peers = landed_ref.shape[0]
    query_cols = query_ref.shape[1] // peers
    for t in range(peers):
        query_ref[:, t * query_cols : (t + 1) * query_cols] = landed_ref[t, :, :query_cols]
        columns = slice(t * HEAD_SIZE, (t + 1) * HEAD_SIZE)
        key_ref[:, columns] = landed_ref[t, :, query_cols : query_cols + HEAD_SIZE]
        value_ref[:, columns] = landed_ref[t, :, query_cols + HEAD_SIZE :]


def on_device(
    queries, key_layout_rows, value_layout_rows, output_gradient, doc_starts, block_mapping
):
    rows_dev, query_cols = queries.shape
    block_count = doc_starts.shape[0]
    block_rows = rows_dev // block_count
    peers = lax.axis_size("tensor")
    axis_length = lax.axis_size("ctx")
    share = rows_dev // peers
    columns = query_cols + 2 * HEAD_SIZE
    low = jnp.bfloat16
    out = jax.ShapeDtypeStruct
    across = [(i, (i + axis_length // 2) % axis_length) for i in range(axis_length)]

    blocks, packed, plan, moved = pl.pallas_call(
        attention_kernel,
        out_shape=(
            out((block_count, block_rows, columns), low),
            out((CAP, block_rows, columns), low),
            out((1 + CAP + block_count,), jnp.int32),
            out((1,), jnp.int32),
        ),
        in_specs=[SMEM, SMEM] + [VMEM] * 4,
        out_specs=(VMEM, VMEM, SMEM, SMEM),
        scratch_shapes=[pltpu.VMEM((rows_dev, HEAD_SIZE), jnp.float32)] * 2,
        name="attention",
    )(
        doc_starts, block_mapping, queries, key_layout_rows, value_layout_rows, output_gradient
    )

    def exchange(count):
        def branch(packed):
            arrived = lax.ppermute(packed[:count], "ctx", across)
            return jnp.pad(arrived, ((0, CAP - count), (0, 0), (0, 0)))

        return branch

    arrived = lax.switch(moved[0], [exchange(count + 1) for count in range(CAP)], packed)
    landed = pl.pallas_call(
        share_kernel,
        out_shape=out((peers, share, columns), low),
        in_specs=[SMEM] + [VMEM] * 2,
        out_specs=VMEM,
        scratch_shapes=[
            pltpu.VMEM((rows_dev, columns), low),
            pltpu.VMEM((2, 2, share, columns // 2), low),
            pltpu.SemaphoreType.DMA((3, 2)),
            pltpu.SemaphoreType.DMA((3, 2)),
        ]
        + [pltpu.SemaphoreType.DMA((2, 2))] * 4,
        compiler_params=pltpu.CompilerParams(
            collective_id=0, has_side_effects=True, vmem_limit_bytes=GRANT
        ),
        name="share",
    )(plan, blocks, arrived)
    return pl.pallas_call(
        assemble_kernel,
        out_shape=(
            out((share, query_cols * peers), low),
            out((share, HEAD_SIZE * peers), low),
            out((share, HEAD_SIZE * peers), low),
        ),
        in_specs=[VMEM],
        out_specs=(VMEM,) * 3,
        compiler_params=pltpu.CompilerParams(vmem_limit_bytes=GRANT),
        name="assemble",
    )(landed)


def solution(mesh):
    return jax.shard_map(
        on_device,
        mesh=mesh,
        in_specs=(
            P("ctx", "tensor"),
            P("ctx", "tensor"),
            P("ctx", "tensor"),
            P("ctx", "tensor"),
            P("ctx"),
            P(),
        ),
        out_specs=(
            P(("ctx", "tensor"), None),
            P(("ctx", "tensor"), None),
            P(("ctx", "tensor"), None),
        ),
        check_vma=False,
    )
```

```python
import jax
import jax.numpy as jnp
from jax import lax
from jax.experimental import pallas as pl
from jax.experimental.pallas import tpu as pltpu
from jax.sharding import PartitionSpec as P

HEAD_SIZE = 128
HIDDEN = -1e30
CAP = 2
HEADS = 2
UNROLL = 4
GRANT = 16 * 2**20
NT = (((1,), (1,)), ((), ()))
NN = (((1,), (0,)), ((), ()))
VMEM = pl.BlockSpec(memory_space=pltpu.VMEM)
SMEM = pl.BlockSpec(memory_space=pltpu.SMEM)
HBM = pl.BlockSpec(memory_space=pltpu.HBM)
MESH = pl.DeviceIdType.MESH


def product(a, b, dims):
    return lax.dot_general(a, b, dims, preferred_element_type=jnp.float32)


def stacked_heads(ref, rows, columns):
    tile = ref[rows, columns]
    return jnp.concatenate(
        [tile[:, h * HEAD_SIZE : (h + 1) * HEAD_SIZE] for h in range(HEADS)], axis=0
    )


def gradients(starts_ref, q_ref, k_ref, v_ref, g_ref, out_ref, key_acc, value_acc):
    query_cols = q_ref.shape[1]
    block_count = starts_ref.shape[0]
    block_rows = q_ref.shape[0] // block_count
    width = HEADS * HEAD_SIZE
    lanes = HEADS * block_rows
    scaling = HEAD_SIZE ** (-0.5)
    key_pos = lax.broadcasted_iota(jnp.int32, (block_rows, lanes), 0)
    query_pos = lax.broadcasted_iota(jnp.int32, (block_rows, lanes), 1) % block_rows
    causal = query_pos >= key_pos
    bias = {}
    for i in range(block_count):
        crossed = jnp.int32(0)
        for j in range(i - 1, -1, -1):
            crossed = crossed + starts_ref[j + 1]
            bias[i, j] = jnp.where(crossed == 0, 0.0, HIDDEN).astype(jnp.float32)
    key_rows = k_ref[...]
    value_rows = v_ref[...]
    key_turned = key_rows.astype(jnp.float32).T.astype(jnp.bfloat16)

    def head_pair(pair, carried):
        columns = pl.ds(pl.multiple_of(pair * width, width), width)
        for i in range(block_count):
            seen = (i + 1) * block_rows
            rows = slice(i * block_rows, seen)
            query = stacked_heads(q_ref, rows, columns)
            grad = stacked_heads(g_ref, rows, columns)
            scores = product(key_rows[:seen], query, NT) * scaling
            dprobs = product(value_rows[:seen], grad, NT)
            masked = [
                scores[j * block_rows : (j + 1) * block_rows] + bias[i, j] for j in range(i)
            ] + [jnp.where(causal, scores[rows], HIDDEN)]
            scores = jnp.concatenate(masked, axis=0)
            raised = jnp.exp(scores - jnp.max(scores, axis=0, keepdims=True))
            weights = raised * (1.0 / jnp.sum(raised, axis=0, keepdims=True))
            delta = jnp.sum(weights * dprobs, axis=0, keepdims=True)
            weights_low = weights.astype(jnp.bfloat16)
            dscores = (weights * (dprobs - delta)).astype(jnp.bfloat16)
            value_acc[:seen, :] += product(weights_low, grad, NN)
            key_acc[:seen, :] += product(dscores, query, NN)
            turned = product(key_turned[:, :seen], dscores, NN) * scaling
            dquery = jnp.concatenate(
                [turned[:, h * block_rows : (h + 1) * block_rows].T for h in range(HEADS)],
                axis=1,
            )
            out_ref[i, :, columns] = dquery.astype(jnp.bfloat16)
        return carried

    lax.fori_loop(0, query_cols // width, head_pair, 0, unroll=UNROLL)
    for i in range(block_count):
        rows = slice(i * block_rows, (i + 1) * block_rows)
        out_ref[i, :, query_cols : query_cols + HEAD_SIZE] = (
            key_acc[rows, :] * scaling
        ).astype(jnp.bfloat16)
        out_ref[i, :, query_cols + HEAD_SIZE :] = value_acc[rows, :].astype(jnp.bfloat16)


def pack(out_ref, packed_ref, plan_ref):
    for j in range(CAP):
        packed_ref[j] = out_ref[plan_ref[1 + j]]


def make_plan(block_count, mapping_ref, plan_ref):
    axis_length = lax.axis_size("ctx")
    position = lax.axis_index("ctx")
    partner = lax.rem(position + axis_length // 2, axis_length)
    zero = jnp.int32(0)
    leaving = zero
    sent = [zero] * CAP
    source = [zero] * block_count
    for s in range(block_count):
        target = mapping_ref[position * block_count + s] - position * block_count
        stays = (target >= 0) & (target < block_count)
        for j in range(CAP):
            sent[j] = jnp.where(stays | (leaving != j), sent[j], s)
        leaving = jnp.where(stays, leaving, leaving + 1)
        for w in range(block_count):
            source[w] = jnp.where(target == w, s, source[w])
    arriving = jnp.int32(block_count)
    for s in range(block_count):
        target = mapping_ref[partner * block_count + s] - position * block_count
        comes = (target >= 0) & (target < block_count)
        for w in range(block_count):
            source[w] = jnp.where(target == w, arriving, source[w])
        arriving = jnp.where(comes, arriving + 1, arriving)
    plan_ref[0] = leaving
    for j in range(CAP):
        plan_ref[1 + j] = sent[j]
    for w in range(block_count):
        plan_ref[1 + CAP + w] = source[w]


def attention_kernel(
    starts_ref, mapping_ref, q_ref, k_ref, v_ref, g_ref,
    out_ref, packed_ref, plan_ref, moved_ref, key_acc, value_acc,
):
    make_plan(starts_ref.shape[0], mapping_ref, plan_ref)
    moved_ref[0] = plan_ref[0] - 1
    key_acc[...] = jnp.zeros_like(key_acc)
    value_acc[...] = jnp.zeros_like(value_acc)
    gradients(starts_ref, q_ref, k_ref, v_ref, g_ref, out_ref, key_acc, value_acc)
    pack(out_ref, packed_ref, plan_ref)


def chosen(own_ref, arrived_ref, place):
    own_count, arrived_count = own_ref.shape[0], arrived_ref.shape[0]
    own = own_ref[jnp.minimum(place, own_count - 1)]
    arrived = arrived_ref[jnp.clip(place - own_count, 0, arrived_count - 1)]
    return jnp.where(place < own_count, own, arrived)


def merge_kernel(plan_ref, own_ref, arrived_ref, out_ref):
    block_count, block_rows, _ = own_ref.shape
    for w in range(block_count):
        rows = slice(w * block_rows, (w + 1) * block_rows)
        out_ref[rows, :] = chosen(own_ref, arrived_ref, plan_ref[1 + CAP + w])


def share_kernel(
    plan_ref, own_ref, arrived_hbm, landed_ref,
    arrived_ref, arrived_sem, stage, relay, near_send, near_recv, first_send, first_recv, last_send, last_recv,
):
    peers, share, columns = landed_ref.shape
    half = columns // 2
    me = lax.axis_index("tensor")
    core = lax.rem(me, 2)
    barrier = pltpu.get_barrier_semaphore()
    for k in range(1, peers):
        pl.semaphore_signal(
            barrier, inc=1, device_id={"tensor": lax.rem(me + k, peers)}, device_id_type=MESH
        )
    fetch = pltpu.make_async_copy(arrived_hbm, arrived_ref, arrived_sem)
    fetch.start()
    fetch.wait()
    merge_kernel(plan_ref, own_ref, arrived_ref, stage)
    pl.semaphore_wait(barrier, peers - 1)

    def device(chips, which):
        return lax.rem(me - core + 2 * chips + peers, peers) + which

    def rows_of(peer):
        return stage.at[pl.ds(pl.multiple_of(peer * share, share), share)]

    def send(source, target, send_sem, recv_sem, to):
        return pltpu.make_async_remote_copy(
            source, target, send_sem, recv_sem, device_id={"tensor": to}, device_id_type=MESH
        )

    ways = ((0, 1), (1, -1))
    cores = (0, 1)
    firsts, nears, lasts = [], [], []
    for w, chips in ways:
        for c in cores:
            firsts.append(
                send(
                    rows_of(device(2, c)).at[:, pl.ds(w * half, half)],
                    relay.at[w, core],
                    first_send.at[w, c],
                    first_recv.at[w, core],
                    device(chips, c),
                )
            )
    for w, chips in ways:
        for c in cores:
            to = device(chips, c)
            nears.append(
                send(rows_of(to), landed_ref.at[me], near_send.at[w, c], near_recv.at[w, core], to)
            )
    other = device(0, 1 - core)
    nears.append(send(rows_of(other), landed_ref.at[me], near_send.at[2, 0], near_recv.at[2, 0], other))
    for copy in firsts + nears:
        copy.start()
    landed_ref[me] = rows_of(me)[...]
    for w, chips in ways:
        for c in cores:
            slot = relay.at[w, c]
            send(slot, slot, first_send.at[w, c], first_recv.at[w, c], other).wait_recv()
            onward = send(
                slot,
                landed_ref.at[device(-chips, c), :, pl.ds(w * half, half)],
                last_send.at[w, c],
                last_recv.at[w, c],
                device(chips, core),
            )
            onward.start()
            lasts.append(onward)
    for copy in firsts + nears + lasts:
        copy.wait_send()
    whole = landed_ref.at[me]
    for w, _ in ways:
        for c in cores:
            send(whole, whole, near_send.at[w, c], near_recv.at[w, c], other).wait_recv()
            send(relay.at[w, c], relay.at[w, c], last_send.at[w, c], last_recv.at[w, c], other).wait_recv()
    send(whole, whole, near_send.at[2, 0], near_recv.at[2, 0], other).wait_recv()


def assemble_kernel(landed_ref, query_ref, key_ref, value_ref):
    peers = landed_ref.shape[0]
    query_cols = query_ref.shape[1] // peers
    for t in range(peers):
        query_ref[:, t * query_cols : (t + 1) * query_cols] = landed_ref[t, :, :query_cols]
        columns = slice(t * HEAD_SIZE, (t + 1) * HEAD_SIZE)
        key_ref[:, columns] = landed_ref[t, :, query_cols : query_cols + HEAD_SIZE]
        value_ref[:, columns] = landed_ref[t, :, query_cols + HEAD_SIZE :]


def on_device(
    queries, key_layout_rows, value_layout_rows, output_gradient, doc_starts, block_mapping
):
    rows_dev, query_cols = queries.shape
    block_count = doc_starts.shape[0]
    block_rows = rows_dev // block_count
    peers = lax.axis_size("tensor")
    axis_length = lax.axis_size("ctx")
    share = rows_dev // peers
    columns = query_cols + 2 * HEAD_SIZE
    low = jnp.bfloat16
    out = jax.ShapeDtypeStruct
    across = [(i, (i + axis_length // 2) % axis_length) for i in range(axis_length)]

    blocks, packed, plan, moved = pl.pallas_call(
        attention_kernel,
        out_shape=(
            out((block_count, block_rows, columns), low),
            out((CAP, block_rows, columns), low),
            out((1 + CAP + block_count,), jnp.int32),
            out((1,), jnp.int32),
        ),
        in_specs=[SMEM, SMEM] + [VMEM] * 4,
        out_specs=(VMEM, VMEM, SMEM, SMEM),
        scratch_shapes=[pltpu.VMEM((rows_dev, HEAD_SIZE), jnp.float32)] * 2,
        name="attention",
    )(
        doc_starts, block_mapping, queries, key_layout_rows, value_layout_rows, output_gradient
    )

    def exchange(count):
        def branch(packed):
            arrived = lax.ppermute(packed[:count], "ctx", across)
            return jnp.pad(arrived, ((0, CAP - count), (0, 0), (0, 0)))

        return branch

    arrived = lax.switch(moved[0], [exchange(count + 1) for count in range(CAP)], packed)
    landed = pl.pallas_call(
        share_kernel,
        out_shape=out((peers, share, columns), low),
        in_specs=[SMEM, VMEM, HBM],
        out_specs=VMEM,
        scratch_shapes=[
            pltpu.VMEM((CAP, block_rows, columns), low),
            pltpu.SemaphoreType.DMA,
            pltpu.VMEM((rows_dev, columns), low),
            pltpu.VMEM((2, 2, share, columns // 2), low),
            pltpu.SemaphoreType.DMA((3, 2)),
            pltpu.SemaphoreType.DMA((3, 2)),
        ]
        + [pltpu.SemaphoreType.DMA((2, 2))] * 4,
        compiler_params=pltpu.CompilerParams(
            collective_id=0, has_side_effects=True, vmem_limit_bytes=GRANT
        ),
        name="share",
    )(plan, blocks, arrived)
    return pl.pallas_call(
        assemble_kernel,
        out_shape=(
            out((share, query_cols * peers), low),
            out((share, HEAD_SIZE * peers), low),
            out((share, HEAD_SIZE * peers), low),
        ),
        in_specs=[VMEM],
        out_specs=(VMEM,) * 3,
        compiler_params=pltpu.CompilerParams(vmem_limit_bytes=GRANT),
        name="assemble",
    )(landed)


def solution(mesh):
    return jax.shard_map(
        on_device,
        mesh=mesh,
        in_specs=(
            P("ctx", "tensor"),
            P("ctx", "tensor"),
            P("ctx", "tensor"),
            P("ctx", "tensor"),
            P("ctx"),
            P(),
        ),
        out_specs=(
            P(("ctx", "tensor"), None),
            P(("ctx", "tensor"), None),
            P(("ctx", "tensor"), None),
        ),
        check_vma=False,
    )
```
